256 devices in a mesh: rows: 16 (over z_lo, y), cols: 16 (over z_hi, x, core).
Axes of the slice: x: 4, y: 4, z: 8 (z_hi: 2, z_lo: 4; z = z_hi * 4 + z_lo), core: 2. Of those that a mesh axis runs over, the one named last changes fastest.
Arguments:
- patches: bfloat16 [384, 384, 1280], P('rows', 'cols'), may hold values from -6 to 6
- conv_taps: float32 [3, 3, 1280], replicated, may hold values from -1.5 to 1.5
- conv_bias: float32 [1280], replicated, may hold values from -3 to 3
- norm_gain: float32 [1280], replicated, may hold values from 0.1 to 1.9
- norm_bias: float32 [1280], replicated, may hold values from -3 to 3
- qkv_weight: bfloat16 [3, 1280, 1280], P(None, None, 'cols'), may hold values from -0.15625 to 0.15625
- qkv_bias: bfloat16 [3, 1280], P(None, 'cols'), may hold values from -3 to 3
Outputs:
- qkv_heads: bfloat16 [3, 16, 384, 30720], P(None, 'cols', 'rows')
The draws below stay inside these ranges and needn't reach their ends.
All inputs are finite; a program needn't handle non-finite values.
Results may differ from the reference program's by a relative error of at most 0.0047.
Values may be sent and summed in bfloat16 or wider, within the bound.
A program may use at most 128 MiB of HBM per device.

```python
import jax
import jax.numpy as jnp
from jax import lax

D = 1280
HEADS = 16
HD = 80
NR = 384
NC = 384


def shard_levels(stream_key, extent, shards, least, largest):
    def one(position, shards_of):
        heights = jax.random.uniform(jax.random.fold_in(jax.random.fold_in(stream_key, 6), position), (shards_of,), jnp.float32, least / len(shards), largest / len(shards))
        return jnp.repeat(jnp.exp(heights), extent[position] // shards_of).reshape((-1,) + (1,) * (len(extent) - position - 1))

    factor_of = one(*shards[0])
    for cut in shards[1:]:
        factor_of = factor_of * one(*cut)
    return factor_of


def gaussian(stream_key, dims, width, limit, split=(), held_as=jnp.bfloat16):
    result = jax.random.normal(stream_key, dims, jnp.float32) * width
    if len(split) > 0:
        result = shard_levels(stream_key, dims, split, -0.22, 0.18) * result
    return jnp.clip(result, min=-limit, max=limit).astype(held_as)


def setup_inputs(seed: int = 0) -> dict:
    key_list = jax.random.split(jax.random.key(seed), 8)
    return {
        "patches": gaussian(key_list[0], (NR, NC, D), 1.0, 6.0, ((0, 16), (1, 16))),
        "conv_taps": gaussian(key_list[1], (3, 3, D), 0.25, 1.5, (), jnp.float32),
        "conv_bias": gaussian(key_list[2], (D,), 0.5, 3.0, (), jnp.float32),
        "norm_gain": jnp.clip(1.0 + 0.18 * jax.random.normal(key_list[3], (D,), jnp.float32), 0.1, 1.9),
        "norm_bias": gaussian(key_list[4], (D,), 0.5, 3.0, (), jnp.float32),
        "qkv_weight": gaussian(key_list[5], (3, D, D), D ** -0.5, 0.15625, ((2, 16),)),
        "qkv_bias": gaussian(key_list[6], (3, D), 0.5, 3.0, ((1, 16),)),
    }


def reference(patches, conv_taps, conv_bias, norm_gain, norm_bias, qkv_weight, qkv_bias):
    padded = jnp.pad(patches, ((1, 1), (1, 1), (0, 0)))
    mixed = patches.astype(jnp.float32) + conv_bias
    for a in range(3):
        for b in range(3):
            mixed = mixed + conv_taps[a, b] * padded[a:a + NR, b:b + NC].astype(jnp.float32)
    mean = lax.optimization_barrier(jnp.mean(mixed, axis=-1, keepdims=True))
    var = lax.optimization_barrier(jnp.mean((mixed - mean) ** 2, axis=-1, keepdims=True))
    normed = ((mixed - mean) / jnp.sqrt(var + 1e-06) * norm_gain + norm_bias).astype(jnp.bfloat16)
    flat = normed.reshape(NR * NC, D)

    def project(pair):
        weight, bias = pair
        out = jnp.dot(flat, weight, preferred_element_type=jnp.float32) + bias.astype(jnp.float32)
        out = out.astype(jnp.bfloat16).reshape(NR, NC, HEADS, HD)
        return jnp.transpose(out, (2, 0, 1, 3)).reshape(HEADS, NR, NC * HD)
    return lax.map(project, (qkv_weight, qkv_bias))
```

```python
import jax
import jax.numpy as jnp
from jax import lax
from jax.sharding import Mesh, PartitionSpec as P

HD = 80
ROWS = ("zl", "y")
COLS = ("zh", "x", "core")
SIDE = ("x", "core")


def with_halo(cells, sides, width):
    for axis, dim in sides:
        count = lax.axis_size(axis)
        ends = count - 1
        head = lax.slice_in_dim(cells, 0, width, axis=dim)
        tail = lax.slice_in_dim(cells, cells.shape[dim] - width, cells.shape[dim], axis=dim)
        cells = jnp.concatenate(
            [
                lax.ppermute(tail, axis, [(i, (i + 1) % count) for i in range(ends)]),
                cells,
                lax.ppermute(head, axis, [((i + 1) % count, i) for i in range(ends)]),
            ],
            axis=dim,
        )
    return cells


def local(patches, conv_taps, conv_bias, norm_gain, norm_bias, qkv_weight, qkv_bias):
    tile_rows, tile_cols, width = patches.shape
    padded = with_halo(patches, ((ROWS, 0), (COLS, 1)), 1)
    mixed = patches.astype(jnp.float32) + conv_bias
    for a in range(3):
        for b in range(3):
            mixed = mixed + conv_taps[a, b] * padded[a : a + tile_rows, b : b + tile_cols].astype(
                jnp.float32
            )
    mean = jnp.mean(mixed, axis=-1, keepdims=True)
    var = jnp.mean((mixed - mean) ** 2, axis=-1, keepdims=True)
    normed = ((mixed - mean) / jnp.sqrt(var + 1e-06) * norm_gain + norm_bias).astype(jnp.bfloat16)
    pair = lax.all_gather(normed, "zh", axis=0, tiled=False)
    weight_side = lax.all_gather(qkv_weight, SIDE, axis=2, tiled=True)
    bias_side = lax.all_gather(qkv_bias, SIDE, axis=1, tiled=True)
    heads = weight_side.shape[2] // HD
    weight_side = weight_side.reshape(3, width, heads, HD)
    bias_side = bias_side.astype(jnp.float32).reshape(3, heads, 1, 1, 1, HD)
    out = jnp.einsum("jrcd,tdhe->thjrce", pair, weight_side, preferred_element_type=jnp.float32)
    out = (out + bias_side).astype(jnp.bfloat16)
    got = lax.all_to_all(out, SIDE, 1, 1, tiled=True)
    got = jnp.transpose(got, (0, 3, 2, 1, 4, 5))
    return got.reshape(3, 1, tile_rows, -1)


def solution(mesh):
    fine = Mesh(mesh.devices.reshape(4, 4, 2, 4, 2), ROWS + COLS)
    placed = (P(ROWS, COLS, None), P(), P(), P(), P(), P(None, None, COLS), P(None, COLS))
    return jax.shard_map(
        local, mesh=fine, in_specs=placed, out_specs=P(None, COLS, ROWS, None), check_vma=False
    )
```

```python
import jax
import jax.numpy as jnp
from jax import lax
from jax.sharding import Mesh, PartitionSpec as P

HD = 80
ROWS = ("zl", "y")
COLS = ("zh", "x", "core")
SIDE = ("x", "core")


def with_halo(cells, sides, width):
    for axis, dim in sides:
        count = lax.axis_size(axis)
        ends = count - 1
        head = lax.slice_in_dim(cells, 0, width, axis=dim)
        tail = lax.slice_in_dim(cells, cells.shape[dim] - width, cells.shape[dim], axis=dim)
        cells = jnp.concatenate(
            [
                lax.ppermute(tail, axis, [(i, (i + 1) % count) for i in range(ends)]),
                cells,
                lax.ppermute(head, axis, [((i + 1) % count, i) for i in range(ends)]),
            ],
            axis=dim,
        )
    return cells


def project(tile, weight_side, bias_side):
    out = jnp.einsum("rcd,tdhe->trhce", tile, weight_side, preferred_element_type=jnp.float32)
    return (out + bias_side).astype(jnp.bfloat16)


def deliver(out):
    return lax.all_to_all(out, SIDE, 2, 2, tiled=True)


def local(patches, conv_taps, conv_bias, norm_gain, norm_bias, qkv_weight, qkv_bias):
    tile_rows, tile_cols, width = patches.shape
    packed = jnp.concatenate([qkv_weight, qkv_bias[:, None, :]], axis=1)
    packed = lax.all_gather(packed, SIDE, axis=2, tiled=True)
    heads = packed.shape[2] // HD
    weight_side = packed[:, :width].reshape(3, width, heads, HD)
    bias_side = packed[:, width].astype(jnp.float32).reshape(3, 1, heads, 1, HD)

    padded = with_halo(patches, ((ROWS, 0), (COLS, 1)), 1)
    mixed = patches.astype(jnp.float32) + conv_bias
    for a in range(3):
        for b in range(3):
            mixed = mixed + conv_taps[a, b] * padded[a : a + tile_rows, b : b + tile_cols].astype(
                jnp.float32
            )
    mean = jnp.mean(mixed, axis=-1, keepdims=True)
    var = jnp.mean((mixed - mean) ** 2, axis=-1, keepdims=True)
    normed = ((mixed - mean) / jnp.sqrt(var + 1e-06) * norm_gain + norm_bias).astype(jnp.bfloat16)
    own = project(normed, weight_side, bias_side)
    normed, own = lax.optimization_barrier((normed, own))
    partner = lax.ppermute(normed, "zh", [(0, 1), (1, 0)])
    own = deliver(own)
    other = deliver(project(partner, weight_side, bias_side))
    first = lax.axis_index("zh") == 0
    low = jnp.where(first, own, other)
    high = jnp.where(first, other, own)
    got = jnp.stack([low, high], axis=2)
    return got.reshape(3, 1, tile_rows, -1)


def solution(mesh):
    fine = Mesh(mesh.devices.reshape(4, 4, 2, 4, 2), ROWS + COLS)
    placed = (P(ROWS, COLS, None), P(), P(), P(), P(), P(None, None, COLS), P(None, COLS))
    return jax.shard_map(
        local, mesh=fine, in_specs=placed, out_specs=P(None, COLS, ROWS, None), check_vma=False
    )
```

```python
import jax
import jax.numpy as jnp
from jax import lax
from jax.sharding import Mesh, PartitionSpec as P

HD = 80
ROWS = ("zl", "y")
COLS = ("zh", "x", "core")
SIDE = ("x", "core")


def with_halo(cells, sides, width):
    for axis, dim in sides:
        count = lax.axis_size(axis)
        ends = count - 1
        head = lax.slice_in_dim(cells, 0, width, axis=dim)
        tail = lax.slice_in_dim(cells, cells.shape[dim] - width, cells.shape[dim], axis=dim)
        cells = jnp.concatenate(
            [
                lax.ppermute(tail, axis, [(i, (i + 1) % count) for i in range(ends)]),
                cells,
                lax.ppermute(head, axis, [((i + 1) % count, i) for i in range(ends)]),
            ],
            axis=dim,
        )
    return cells


def project(tile, weight_side, bias_side):
    out = jnp.einsum("rcd,tdhe->trhce", tile, weight_side, preferred_element_type=jnp.float32)
    out = (out + bias_side).astype(jnp.bfloat16)
    return out.reshape(out.shape[:3] + (-1,))


def deliver(out):
    return lax.all_to_all(out, SIDE, 2, 2, tiled=True)


def local(patches, conv_taps, conv_bias, norm_gain, norm_bias, qkv_weight, qkv_bias):
    tile_rows, tile_cols, width = patches.shape
    packed = jnp.concatenate([qkv_weight, qkv_bias[:, None, :]], axis=1)
    packed = lax.all_gather(packed, SIDE, axis=2, tiled=True)
    heads = packed.shape[2] // HD
    weight_side = packed[:, :width].reshape(3, width, heads, HD)
    bias_side = packed[:, width].astype(jnp.float32).reshape(3, 1, heads, 1, HD)

    padded = with_halo(patches, ((ROWS, 0), (COLS, 1)), 1)
    mixed = patches.astype(jnp.float32) + conv_bias
    for a in range(3):
        for b in range(3):
            mixed = mixed + conv_taps[a, b] * padded[a : a + tile_rows, b : b + tile_cols].astype(
                jnp.float32
            )
    mean = jnp.mean(mixed, axis=-1, keepdims=True)
    var = jnp.mean((mixed - mean) ** 2, axis=-1, keepdims=True)
    normed = ((mixed - mean) / jnp.sqrt(var + 1e-06) * norm_gain + norm_bias).astype(jnp.bfloat16)
    partner = lax.ppermute(normed, "zh", [(0, 1), (1, 0)])
    own = project(normed, weight_side, bias_side)
    weight_late, bias_late, own = lax.optimization_barrier((weight_side, bias_side, own))
    own = deliver(own)
    other = deliver(project(partner, weight_late, bias_late))
    me = lax.axis_index("zh")
    got = jnp.zeros(own.shape[:2] + (2,) + own.shape[2:], own.dtype)
    got = lax.dynamic_update_slice_in_dim(got, own[:, :, None], me, axis=2)
    got = lax.dynamic_update_slice_in_dim(got, other[:, :, None], 1 - me, axis=2)
    return got.reshape(3, 1, tile_rows, -1)


def solution(mesh):
    fine = Mesh(mesh.devices.reshape(4, 4, 2, 4, 2), ROWS + COLS)
    placed = (P(ROWS, COLS, None), P(), P(), P(), P(), P(None, None, COLS), P(None, COLS))
    return jax.shard_map(
        local, mesh=fine, in_specs=placed, out_specs=P(None, COLS, ROWS, None), check_vma=False
    )
```
